128 devices in a mesh: tmpl: 16 (over x, y), sta: 8 (over z, core).
Axes of the slice: x: 4, y: 4, z: 4, core: 2. Of those that a mesh axis runs over, the one named last changes fastest.
Arguments:
- waveforms: bfloat16 [6144, 9088], P(('tmpl', 'sta'))
- template_taps: bfloat16 [24576, 400], P(('tmpl', 'sta')), may hold values from -6 to 6
- slot_template: int32 [24576], P(('tmpl', 'sta')), may hold values from 0 to 127
- slot_channel: int32 [24576], P(('tmpl', 'sta')), may hold values from 0 to 6143, as said below
- slot_moveout: int32 [24576], P(('tmpl', 'sta')), may hold values from 0 to 383
Outputs:
- stacks: float32 [8192, 2048], P('sta', 'tmpl')
The draws below stay inside these ranges and needn't reach their ends.
Inputs may be any that keep to these rules, and one draw needn't show every extreme that they name: Entry s lies in the station group of its aligned block b = s // 192 of entries: (slot_channel[s] // 48) % 8 equals b % 8. Within one aligned block, the entries take at most 8 distinct channels from any one block of 48 channels (c // 48 equal), and in every aligned block some block of channels gives exactly 8.
All inputs are finite; a program needn't handle non-finite values.
Results may differ from the reference program's by a relative error of at most 0.0029.
Values may be sent and summed in bfloat16 or wider, within the bound.
A program may use at most 128 MiB of HBM per device.

```python
import math
import jax
import jax.numpy as jnp
from jax import lax

TAPS = 400
CH_TPL = 30
MOVE = 384
LAGS = 8192
SLOT_DEV = 192
TPL_DEV = 128
CH_DEV = 48
CAP = 8
SAMPLES = 9088
CHANNELS = 6144
SLOTS = 24576
TEMPLATES = 2048
N_TMPL = 16
N_STA = 8


def draw_waveforms(key, part):
    subkeys = jax.random.split(jax.random.fold_in(key, 3), 3)
    chan_scale = jnp.exp(jax.random.uniform(subkeys[0], (CHANNELS, 1), jnp.float32, 0.0, math.log(10.0)))
    time_scale = jnp.exp(jax.random.uniform(subkeys[1], (1, SAMPLES), jnp.float32, 0.0, math.log(10.0)))
    values = jax.random.normal(subkeys[2], (CHANNELS, SAMPLES), jnp.float32) * chan_scale * time_scale
    return values.astype(jnp.bfloat16)


def draw_slot_channel(key, part):
    subkeys = jax.random.split(jax.random.fold_in(key, 17), 6)
    blocks_all = N_TMPL * N_STA
    counts = jax.random.randint(subkeys[0], (blocks_all, N_TMPL), 2, CAP + 1)
    busiest = jax.random.randint(subkeys[1], (blocks_all, 1), 0, N_TMPL)
    owner_row = jnp.arange(N_TMPL, dtype=jnp.int32)[None, :]
    counts = jnp.where(owner_row == busiest, CAP, counts)
    offsets = jax.random.randint(subkeys[2], (blocks_all, N_TMPL), 0, CH_DEV)
    position = jnp.arange(SLOT_DEV, dtype=jnp.int32)[None, :]
    cover_owner = jnp.broadcast_to(jnp.minimum(position // CAP, N_TMPL - 1), (blocks_all, SLOT_DEV))
    cover_rank = jnp.broadcast_to(position % CAP, (blocks_all, SLOT_DEV))
    cover_count = jnp.take_along_axis(counts, cover_owner, axis=1)
    covering = (position < N_TMPL * CAP) & (cover_rank < cover_count)
    random_owner = jax.random.randint(subkeys[3], (blocks_all, SLOT_DEV), 0, N_TMPL)
    random_raw = jax.random.randint(subkeys[4], (blocks_all, SLOT_DEV), 0, CAP)
    owner_ids = jnp.where(covering, cover_owner, random_owner)
    owner_count = jnp.take_along_axis(counts, owner_ids, axis=1)
    slot_rank = jnp.where(covering, cover_rank, random_raw % owner_count)
    scores = jax.random.randint(subkeys[5], (blocks_all, SLOT_DEV), 0, 1 << 20) * SLOT_DEV + position
    shuffle = jnp.argsort(scores, axis=1, stable=True)
    owner_ids = jnp.take_along_axis(owner_ids, shuffle, axis=1)
    slot_rank = jnp.take_along_axis(slot_rank, shuffle, axis=1)
    group_ids = (jnp.arange(blocks_all, dtype=jnp.int32) % N_STA)[:, None]
    local_ids = (jnp.take_along_axis(offsets, owner_ids, axis=1) + slot_rank) % CH_DEV
    channel_ids = (owner_ids * N_STA + group_ids) * CH_DEV + local_ids
    return channel_ids.reshape(SLOTS).astype(jnp.int32)


def plant(array, rng, smallest, largest):
    longest = array.shape.index(max(array.shape))
    spots = []
    for shift in (0, 1):
        where = [jax.random.randint(jax.random.fold_in(rng, axis), (), 0, length) for axis, length in enumerate(array.shape)]
        where[longest] = (where[longest] + shift) % array.shape[longest]
        spots.append(tuple(where))
    return array.at[spots[0]].set(smallest).at[spots[1]].set(largest)


def steps_of(stream_key, shape, cuts, smallest, high):
    loudness = 1.0
    for axis_at, blocks in cuts:
        heights = jax.random.uniform(jax.random.fold_in(jax.random.fold_in(stream_key, 6), axis_at), (blocks,), jnp.float32, smallest / len(cuts), high / len(cuts))
        loudness = loudness * jnp.repeat(jnp.exp(heights), shape[axis_at] // blocks).reshape((-1,) + (1,) * (len(shape) - 1 - axis_at))
    return loudness


def normal_values(rng, extent, deviation, bound, shards=(), kind=jnp.bfloat16):
    drawn = deviation * jax.random.normal(rng, extent, jnp.float32)
    if shards:
        drawn = drawn * steps_of(rng, extent, shards, -0.22, 0.18)
    return jnp.clip(drawn, -bound, bound).astype(kind)


def setup_inputs(seed: int = 0) -> dict:
    key_list = jax.random.split(jax.random.key(seed), 6)
    waveforms = draw_waveforms(jax.random.fold_in(key_list[5], 71), 0)
    template_taps = normal_values(key_list[1], (SLOTS, TAPS), 1.0, 6.0, ((0, 128),))
    slot_template = plant(jax.random.randint(key_list[2], (SLOTS,), 0, TPL_DEV), jax.random.fold_in(key_list[2], 1), 0, TPL_DEV - 1).astype(jnp.int32)
    slot_channel = draw_slot_channel(jax.random.fold_in(key_list[5], 71), 0)
    slot_moveout = plant(jax.random.randint(key_list[4], (SLOTS,), 0, MOVE), jax.random.fold_in(key_list[4], 1), 0, MOVE - 1).astype(jnp.int32)
    return dict(waveforms=waveforms, template_taps=template_taps, slot_template=slot_template, slot_channel=slot_channel, slot_moveout=slot_moveout)


def frames_of(signal, lag_blocks, span_blocks):
    pieces = signal.reshape(signal.shape[0], lag_blocks + span_blocks - 1, 128)
    return jnp.concatenate([pieces[:, offset:offset + lag_blocks] for offset in range(span_blocks)], axis=-1)

def toeplitz(tap_rows, span_blocks):
    span_width = span_blocks * 128
    padded = jnp.concatenate([tap_rows, jnp.zeros((tap_rows.shape[0], span_width + 1 - tap_rows.shape[1]), tap_rows.dtype)], axis=1)
    tiled = jnp.tile(padded, (1, 128))[:, :128 * span_width]
    return tiled.reshape(tap_rows.shape[0], 128, span_width)

def band_matrix(span_blocks, tap_count, dtype):
    column = jnp.arange(span_blocks * 128, dtype=jnp.int32)[:, None]
    lagged = jnp.arange(128, dtype=jnp.int32)[None, :]
    return ((column >= lagged) & (column < lagged + tap_count)).astype(dtype)

def reference(waveforms, template_taps, slot_template, slot_channel, slot_moveout):
    eps = 1e-06
    span_blocks = (TAPS + 127) // 128 + 1
    lag_blocks = LAGS // 128
    seg_length = LAGS + (span_blocks - 1) * 128
    scale = math.sqrt(TAPS / CH_TPL)
    per_block = 256
    band = band_matrix(span_blocks, TAPS, jnp.float32)
    positions = jnp.arange(SLOTS, dtype=jnp.int32)
    tmpl_index = (positions // (SLOT_DEV * N_STA) * TPL_DEV + slot_template).astype(jnp.int32)
    scan_inputs = (slot_channel.reshape(-1, per_block), slot_moveout.reshape(-1, per_block), template_taps.reshape(-1, per_block, TAPS), tmpl_index.reshape(-1, per_block))

    def one_block(stack, pieces):
        channel_ids, moveouts, tap_rows, template_ids = pieces
        picked = waveforms[channel_ids].astype(jnp.float32)
        segment = jax.vmap(lambda signal, offset: lax.dynamic_slice_in_dim(signal, offset, seg_length))(picked, moveouts)
        squares = lax.optimization_barrier((segment * segment).astype(jnp.bfloat16)).astype(jnp.float32)
        framed = frames_of(segment, lag_blocks, span_blocks)
        framed_sq = frames_of(squares, lag_blocks, span_blocks)
        taps_float = tap_rows.astype(jnp.float32)
        corr = jnp.einsum('bqu,bru->bqr', framed, toeplitz(taps_float, span_blocks), precision=lax.Precision.HIGHEST)
        energy = jnp.einsum('bqu,ur->bqr', framed_sq, band, precision=lax.Precision.HIGHEST)
        tap_energy = lax.optimization_barrier(jnp.sum(taps_float * taps_float, axis=1))
        normed = scale * corr * lax.rsqrt(tap_energy + eps)[:, None, None] * lax.rsqrt(energy + eps)
        normed = lax.optimization_barrier(normed.astype(jnp.bfloat16)).astype(jnp.float32)
        stack = stack.at[template_ids].add(normed.reshape(per_block, LAGS))
        return (stack, None)
    initial = jnp.zeros((TEMPLATES, LAGS), jnp.float32)
    stack, leftover = lax.scan(one_block, initial, scan_inputs)
    return stack.T
```

```python
import functools
import math

import jax
import jax.numpy as jnp
from jax import lax
from jax.experimental import pallas as pl
from jax.experimental.pallas import tpu as pltpu
from jax.sharding import PartitionSpec as P

TAPS = 400
CH_TPL = 30
LAGS = 8192
TPL_DEV = 128
CAP = 8
EPS = 1e-06
SCALE = math.sqrt(TAPS / CH_TPL)
LANES = 128
SPAN = 5
LAG_BLOCKS = LAGS // LANES
ROWS = 72
MESH = pl.DeviceIdType.MESH

OFFSETS = (
    (1, 0), (3, 0), (0, 1), (0, 3), (1, 1), (3, 3), (1, 3), (3, 1),
    (2, 0), (0, 2), (2, 1), (1, 2), (2, 3), (3, 2), (2, 2),
)


def plan_rows(slot_channel, channels_here, owners, groups):
    owner = slot_channel // channels_here // groups
    local = slot_channel % channels_here
    key = owner * channels_here + local
    count = key.shape[0]
    order = jnp.arange(count, dtype=jnp.int32)
    earlier = (key[:, None] == key[None, :]) & (order[None, :] < order[:, None])
    first = ~jnp.any(earlier, axis=1)
    below = (owner[:, None] == owner[None, :]) & (key[None, :] < key[:, None]) & first[None, :]
    row = owner * CAP + jnp.sum(below.astype(jnp.int32), axis=1)
    hit = (row[:, None] == jnp.arange(owners * CAP, dtype=jnp.int32)[None, :]) & first[:, None]
    request = jnp.sum(jnp.where(hit, local[:, None], 0), axis=0)
    return request, row


def fetch_kernel(req_smem, req_ref, wave_ref, out_ref, req_all, send, req_here, req_send, req_recv, data_send, data_recv, local_sem):
    me = lax.axis_index("tmpl")
    x, y = me // 4, me % 4
    peers = [((x + dx) % 4) * 4 + (y + dy) % 4 for dx, dy in OFFSETS]
    sources = [((x + 4 - dx) % 4) * 4 + (y + 4 - dy) % 4 for dx, dy in OFFSETS]
    count = len(peers)

    barrier = pltpu.get_barrier_semaphore()
    for peer in peers:
        pl.semaphore_signal(barrier, inc=1, device_id={"tmpl": peer}, device_id_type=MESH)
    pl.semaphore_wait(barrier, count)

    asks = []
    for d, peer in enumerate(peers):
        copy = pltpu.make_async_remote_copy(
            src_ref=req_ref,
            dst_ref=req_all.at[d],
            send_sem=req_send.at[d],
            recv_sem=req_recv.at[d],
            device_id={"tmpl": peer},
            device_id_type=MESH,
        )
        copy.start()
        asks.append(copy)
    for k in range(CAP):
        out_ref[me * CAP + k] = wave_ref[req_smem[0, me * CAP + k]]
    for copy in asks:
        copy.wait()
    here = pltpu.make_async_copy(req_all, req_here, local_sem)
    here.start()
    here.wait()

    sends = []
    for d in range(count):
        back = OFFSETS.index(((4 - OFFSETS[d][0]) % 4, (4 - OFFSETS[d][1]) % 4))
        for k in range(CAP):
            send[d * CAP + k] = wave_ref[req_here[back, 0, me * CAP + k]]
        copy = pltpu.make_async_remote_copy(
            src_ref=send.at[pl.ds(d * CAP, CAP)],
            dst_ref=out_ref.at[pl.ds(me * CAP, CAP)],
            send_sem=data_send.at[d],
            recv_sem=data_recv.at[d],
            device_id={"tmpl": peers[d]},
            device_id_type=MESH,
        )
        copy.start()
        sends.append(copy)
    for copy in sends:
        copy.wait()


def fetch(request, waves, owners):
    blocks = waves.shape[1] // LANES
    waves = jnp.pad(waves.reshape(waves.shape[0], blocks, LANES), ((0, 0), (0, ROWS - blocks), (0, 0)))
    wide = jnp.broadcast_to(request[None, :], (8, request.shape[0]))
    peers = owners - 1
    return pl.pallas_call(
        fetch_kernel,
        out_shape=jax.ShapeDtypeStruct((owners * CAP, ROWS, LANES), jnp.bfloat16),
        in_specs=[
            pl.BlockSpec(memory_space=pltpu.SMEM),
            pl.BlockSpec(memory_space=pltpu.VMEM),
            pl.BlockSpec(memory_space=pltpu.VMEM),
        ],
        out_specs=pl.BlockSpec(memory_space=pltpu.VMEM),
        scratch_shapes=[
            pltpu.VMEM((peers, 8, LANES), jnp.int32),
            pltpu.VMEM((peers * CAP, ROWS, LANES), jnp.bfloat16),
            pltpu.SMEM((peers, 8, LANES), jnp.int32),
            pltpu.SemaphoreType.DMA((peers,)),
            pltpu.SemaphoreType.DMA((peers,)),
            pltpu.SemaphoreType.DMA((peers,)),
            pltpu.SemaphoreType.DMA((peers,)),
            pltpu.SemaphoreType.DMA,
        ],
        compiler_params=pltpu.CompilerParams(collective_id=0, has_side_effects=True),
        name="fetch",
    )(wide, wide, waves)


def correlate_kernel(row_ref, move_ref, core_ref, wave_ref, taps_ref, label_ref, send_ref, keep_ref, frames, inv, band, flipped, norm, toep0, toep1, wide0, wide1, roll0, roll1, ncc):
    channels = wave_ref.shape[0]
    slots = taps_ref.shape[0]
    sub = lax.broadcasted_iota(jnp.int32, (LANES, LANES), 0)
    lane = lax.broadcasted_iota(jnp.int32, (LANES, LANES), 1)

    column = lax.broadcasted_iota(jnp.int32, (SPAN * LANES, LANES), 0)
    lagged = lax.broadcasted_iota(jnp.int32, (SPAN * LANES, LANES), 1)
    band[...] = jnp.where((column >= lagged) & (column < lagged + TAPS), 1.0, 0.0).astype(jnp.bfloat16)
    flip = jnp.where(sub == (LANES - lane) % LANES, 1.0, 0.0).astype(jnp.bfloat16)
    power = jnp.zeros((slots, 1), jnp.float32)
    for b in range(4):
        piece = taps_ref[:, b * LANES : (b + 1) * LANES]
        flipped[b] = jnp.dot(piece, flip, preferred_element_type=jnp.float32)
        piece = piece.astype(jnp.float32)
        power = power + jnp.sum(piece * piece, axis=1, keepdims=True)
    norm[...] = jnp.broadcast_to(SCALE * lax.rsqrt(power + EPS), (slots, LANES))

    for wide in (wide0, wide1):
        wide[ROWS:, :] = jnp.zeros((8, LANES), jnp.float32)

    def channel_pair(i, carry):
        for p, wide in enumerate((wide0, wide1)):
            c = 2 * i + p
            wide[:ROWS, :] = wave_ref[c].astype(jnp.float32)
            frame = jnp.concatenate([wide[a : a + ROWS, :] for a in range(SPAN)], axis=1)
            frames[c] = frame.astype(jnp.bfloat16)
            squares = (frame * frame).astype(jnp.bfloat16)
            energy = jnp.dot(squares, band[...], preferred_element_type=jnp.float32)
            inv[c] = lax.rsqrt(energy + EPS)
        return carry

    lax.fori_loop(0, channels // 2, channel_pair, 0)

    lower = lane <= sub
    edge = lax.broadcasted_iota(jnp.int32, (LAG_BLOCKS, LANES), 1)

    def slot_pair(i, carry):
        for p, (toep, rolled) in enumerate(((toep0, roll0), (toep1, roll1))):
            s = 2 * i + p
            row = row_ref[s]
            move = move_ref[s]
            coarse = move // LANES
            fine = move % LANES
            last = jnp.zeros((LANES, LANES), jnp.float32)
            for b in range(4):
                circ = jnp.broadcast_to(flipped[b, pl.ds(s, 1), :], (LANES, LANES))
                circ = pltpu.roll(circ, 0, 1, stride=1, stride_axis=0)
                toep[b * LANES : (b + 1) * LANES, :] = jnp.where(lower, circ, last).astype(jnp.bfloat16)
                last = circ
            toep[4 * LANES :, :] = jnp.where(lower, 0.0, last).astype(jnp.bfloat16)
            corr = jnp.dot(frames[row], toep[...], preferred_element_type=jnp.float32)
            normed = corr * jnp.broadcast_to(norm[pl.ds(s, 1), :], corr.shape) * inv[row]
            normed = normed.astype(jnp.bfloat16).astype(jnp.float32)
            rolled[...] = pltpu.roll(normed, (LANES - fine) % LANES, 1)
            near = rolled[pl.ds(coarse, LAG_BLOCKS), :]
            far = rolled[pl.ds(coarse + 1, LAG_BLOCKS), :]
            ncc[pl.ds(s * LAG_BLOCKS, LAG_BLOCKS), :] = jnp.where(edge < LANES - fine, near, far)
        return carry

    lax.fori_loop(0, slots // 2, slot_pair, 0)

    core = core_ref[0]

    def block(i, carry):
        z, q = i // 8, i % 8
        for h in range(2):
            at = (2 * z + (core + h) % 2) * 8 + q
            picked = ncc[pl.ds(at, slots, stride=LAG_BLOCKS), :].astype(jnp.bfloat16)
            total = jnp.dot(label_ref[...], picked, preferred_element_type=jnp.float32)
            if h == 0:
                keep_ref[i] = total
            else:
                send_ref[i] = total.astype(jnp.bfloat16)
        return carry

    lax.fori_loop(0, LAG_BLOCKS // 2, block, 0)


def correlate(rows, moveouts, core, source, taps, templates):
    slots = taps.shape[0]
    channels = source.shape[0]
    taps = jnp.pad(taps, ((0, 0), (0, 4 * LANES - TAPS)))
    label = (jnp.arange(TPL_DEV, dtype=jnp.int32)[:, None] == templates[None, :]).astype(jnp.bfloat16)
    half = LAG_BLOCKS // 2
    vmem = pl.BlockSpec(memory_space=pltpu.VMEM)
    smem = pl.BlockSpec(memory_space=pltpu.SMEM)
    return pl.pallas_call(
        correlate_kernel,
        out_shape=(
            jax.ShapeDtypeStruct((half, TPL_DEV, LANES), jnp.bfloat16),
            jax.ShapeDtypeStruct((half, TPL_DEV, LANES), jnp.float32),
        ),
        in_specs=[smem, smem, smem, vmem, vmem, vmem],
        out_specs=(vmem, vmem),
        scratch_shapes=[
            pltpu.VMEM((channels, ROWS, SPAN * LANES), jnp.bfloat16),
            pltpu.VMEM((channels, ROWS, LANES), jnp.float32),
            pltpu.VMEM((SPAN * LANES, LANES), jnp.bfloat16),
            pltpu.VMEM((4, slots, LANES), jnp.float32),
            pltpu.VMEM((slots, LANES), jnp.float32),
            pltpu.VMEM((SPAN * LANES, LANES), jnp.bfloat16),
            pltpu.VMEM((SPAN * LANES, LANES), jnp.bfloat16),
            pltpu.VMEM((ROWS + 8, LANES), jnp.float32),
            pltpu.VMEM((ROWS + 8, LANES), jnp.float32),
            pltpu.VMEM((ROWS, LANES), jnp.float32),
            pltpu.VMEM((ROWS, LANES), jnp.float32),
            pltpu.VMEM((slots * LAG_BLOCKS, LANES), jnp.float32),
        ],
        compiler_params=pltpu.CompilerParams(vmem_limit_bytes=56 << 20),
        name="correlate",
    )(rows, moveouts, core, source, taps, label)


def combine_kernel(send_ref, keep_ref, out_ref, near, far, outgoing, near_send, near_recv, far_send, far_recv):
    me = lax.axis_index("sta")
    z, core = me // 2, me % 2
    partner = z * 2 + (core + 1) % 2
    others = [(z + step) % 4 for step in (2, 1, 3)]

    barrier = pltpu.get_barrier_semaphore()
    for peer in [partner] + [other * 2 + core for other in others]:
        pl.semaphore_signal(barrier, inc=1, device_id={"sta": peer}, device_id_type=MESH)
    pl.semaphore_wait(barrier, 4)

    firsts = []
    for n, other in enumerate(others + [z]):
        copy = pltpu.make_async_remote_copy(
            src_ref=send_ref.at[pl.ds(other * 8, 8)],
            dst_ref=near.at[n],
            send_sem=near_send.at[n],
            recv_sem=near_recv.at[n],
            device_id={"sta": partner},
            device_id_type=MESH,
        )
        copy.start()
        firsts.append(copy)
    seconds = []
    for n, other in enumerate(others):
        firsts[n].wait()
        for q in range(8):
            outgoing[n, q] = (keep_ref[other * 8 + q] + near[n, q].astype(jnp.float32)).astype(jnp.bfloat16)
        copy = pltpu.make_async_remote_copy(
            src_ref=outgoing.at[n],
            dst_ref=far.at[n],
            send_sem=far_send.at[n],
            recv_sem=far_recv.at[n],
            device_id={"sta": other * 2 + core},
            device_id_type=MESH,
        )
        copy.start()
        seconds.append(copy)
    firsts[3].wait()
    for copy in seconds:
        copy.wait()
    for q in range(8):
        total = keep_ref[z * 8 + q] + near[3, q].astype(jnp.float32)
        for n in range(3):
            total = total + far[n, q].astype(jnp.float32)
        out_ref[q * LANES : (q + 1) * LANES, :] = total.T


def combine(send, keep):
    vmem = pl.BlockSpec(memory_space=pltpu.VMEM)
    return pl.pallas_call(
        combine_kernel,
        out_shape=jax.ShapeDtypeStruct((8 * LANES, TPL_DEV), jnp.float32),
        in_specs=[vmem, vmem],
        out_specs=vmem,
        scratch_shapes=[
            pltpu.VMEM((4, 8, TPL_DEV, LANES), jnp.bfloat16),
            pltpu.VMEM((3, 8, TPL_DEV, LANES), jnp.bfloat16),
            pltpu.VMEM((3, 8, TPL_DEV, LANES), jnp.bfloat16),
            pltpu.SemaphoreType.DMA((4,)),
            pltpu.SemaphoreType.DMA((4,)),
            pltpu.SemaphoreType.DMA((3,)),
            pltpu.SemaphoreType.DMA((3,)),
        ],
        compiler_params=pltpu.CompilerParams(collective_id=1, has_side_effects=True),
        name="combine",
    )(send, keep)


def per_device(waveforms, template_taps, slot_template, slot_channel, slot_moveout):
    groups = lax.axis_size("sta")
    owners = lax.axis_size("tmpl")
    request, rows = plan_rows(slot_channel, waveforms.shape[0], owners, groups)
    source = fetch(request, waveforms, owners)
    core = (lax.axis_index("sta") % 2).astype(jnp.int32).reshape(1)
    send, keep = correlate(rows, slot_moveout, core, source, template_taps, slot_template)
    return combine(send, keep)


def solution(mesh):
    return jax.shard_map(
        per_device,
        mesh=mesh,
        in_specs=(
            P(("tmpl", "sta"), None),
            P(("tmpl", "sta"), None),
            P(("tmpl", "sta")),
            P(("tmpl", "sta")),
            P(("tmpl", "sta")),
        ),
        out_specs=P("sta", "tmpl"),
        check_vma=False,
    )
```

```python
import functools
import math

import jax
import jax.numpy as jnp
from jax import lax
from jax.experimental import pallas as pl
from jax.experimental.pallas import tpu as pltpu
from jax.sharding import PartitionSpec as P

TAPS = 400
CH_TPL = 30
LAGS = 8192
TPL_DEV = 128
CAP = 8
EPS = 1e-06
SCALE = math.sqrt(TAPS / CH_TPL)
LANES = 128
SPAN = 5
DEPTH = 528
LAG_BLOCKS = LAGS // LANES
BLOCKS = 71
ROWS = 72
PITCH = LAG_BLOCKS + 1
EARLY = 32
MESH = pl.DeviceIdType.MESH


def plan_rows(slot_channel, channels_here, owners, groups):
    owner = slot_channel // channels_here // groups
    local = slot_channel % channels_here
    key = owner * channels_here + local
    count = key.shape[0]
    order = jnp.arange(count, dtype=jnp.int32)
    earlier = (key[:, None] == key[None, :]) & (order[None, :] < order[:, None])
    first = ~jnp.any(earlier, axis=1)
    below = (owner[:, None] == owner[None, :]) & (key[None, :] < key[:, None]) & first[None, :]
    row = owner * CAP + jnp.sum(below.astype(jnp.int32), axis=1)
    hit = (row[:, None] == jnp.arange(owners * CAP, dtype=jnp.int32)[None, :]) & first[:, None]
    request = jnp.sum(jnp.where(hit, local[:, None], 0), axis=0)
    return request, row


def stack_kernel(
    req_smem, row_ref, move_ref, req_ref, wave_ref, taps_ref, tmpl_ref, out_ref,
    req_all, send, recv, wave32, inv, band, flipped, norm, toep, squares, roll0, roll1, roll2, roll3, ncc, label,
    near_out, near, far_out, far, keep, req_here,
    req_send, req_recv, data_send, data_recv, near_send, near_recv, far_send, far_recv, local_sem,
):
    slots = taps_ref.shape[0]
    me = lax.axis_index("tmpl")
    x, y = me // 4, me % 4
    group = lax.axis_index("sta")
    z, core = group // 2, group % 2
    partner = z * 2 + (core + 1) % 2
    steps = (2, 1, 3)
    count = 16

    def peer(d):
        return ((x + d // 4) % 4) * 4 + (y + d % 4) % 4

    def source(d):
        return ((x + 4 - d // 4) % 4) * 4 + (y + 4 - d % 4) % 4

    barrier = pltpu.get_barrier_semaphore()
    for d in range(1, count):
        pl.semaphore_signal(barrier, inc=1, device_id={"tmpl": peer(d)}, device_id_type=MESH)
    for other in [partner] + [((z + step) % 4) * 2 + core for step in steps]:
        pl.semaphore_signal(barrier, inc=1, device_id={"sta": other}, device_id_type=MESH)

    sub = lax.broadcasted_iota(jnp.int32, (LANES, LANES), 0)
    lane = lax.broadcasted_iota(jnp.int32, (LANES, LANES), 1)
    flip = jnp.where(sub == (LANES - lane) % LANES, 1.0, 0.0).astype(jnp.bfloat16)
    power = jnp.zeros((slots, 1), jnp.float32)
    for b in range(4):
        piece = taps_ref[:, b * LANES : min(b * LANES + LANES, TAPS)]
        wide = piece.shape[1]
        flipped[b] = jnp.dot(piece, flip[:wide, :], preferred_element_type=jnp.float32)
        piece = piece.astype(jnp.float32)
        power = power + jnp.sum(piece * piece, axis=1, keepdims=True)
    norm[...] = jnp.broadcast_to(SCALE * lax.rsqrt(power + EPS), (slots, LANES))
    pl.semaphore_wait(barrier, count - 1 + 4)

    def ask(d):
        return pltpu.make_async_remote_copy(
            src_ref=req_ref,
            dst_ref=req_all.at[d],
            send_sem=req_send.at[d],
            recv_sem=req_recv.at[d],
            device_id={"tmpl": peer(d)},
            device_id_type=MESH,
        )

    for d in range(1, count):
        ask(d).start()

    lower = lane <= sub

    def build(s):
        last = jnp.zeros((LANES, LANES), jnp.float32)
        for b in range(4):
            circ = jnp.broadcast_to(flipped[b, pl.ds(s, 1), :], (LANES, LANES))
            circ = pltpu.roll(circ, 0, 1, stride=1, stride_axis=0)
            toep[s, b * LANES : (b + 1) * LANES, :] = jnp.where(lower, circ, last).astype(jnp.bfloat16)
            last = circ
        tail = DEPTH - 4 * LANES
        toep[s, 4 * LANES :, :] = jnp.where(lower[:tail], 0.0, last[:tail]).astype(jnp.bfloat16)

    def build_pair(i, carry):
        build(2 * i)
        build(2 * i + 1)
        return carry

    lax.fori_loop(0, EARLY // 2, build_pair, 0)

    for k in range(CAP):
        recv[me * CAP + k] = wave_ref[req_smem[0, me * CAP + k]]
    for d in range(1, count):
        ask(d).wait()
    here = pltpu.make_async_copy(req_all, req_here, local_sem)
    here.start()
    here.wait()

    def data(d, owner):
        return pltpu.make_async_remote_copy(
            src_ref=send.at[d],
            dst_ref=recv.at[pl.ds(owner * CAP, CAP)],
            send_sem=data_send.at[d],
            recv_sem=data_recv.at[d],
            device_id={"tmpl": peer(d)},
            device_id_type=MESH,
        )

    for d in range(1, count):
        back = (4 - d // 4) % 4 * 4 + (4 - d % 4) % 4
        for k in range(CAP):
            send[d, k] = wave_ref[req_here[back, 0, me * CAP + k]]
        data(d, me).start()

    lax.fori_loop(EARLY // 2, slots // 2, build_pair, 0)

    column = lax.broadcasted_iota(jnp.int32, (DEPTH, LANES), 0)
    lagged = lax.broadcasted_iota(jnp.int32, (DEPTH, LANES), 1)
    band[...] = jnp.where((column >= lagged) & (column < lagged + TAPS), 1.0, 0.0).astype(jnp.bfloat16)
    wave32[:, ROWS:, :] = jnp.zeros((wave32.shape[0], wave32.shape[1] - ROWS, LANES), jnp.float32)

    def energies(c):
        for p in range(4):
            wave32[c + p, :BLOCKS, :] = recv[c + p].astype(jnp.float32)
            for a in range(SPAN):
                width = min(LANES, DEPTH - a * LANES)
                frame = wave32[c + p, a : a + ROWS, :width].astype(jnp.bfloat16)
                squares[p * ROWS : (p + 1) * ROWS, a * LANES : a * LANES + width] = frame * frame
        energy = jnp.dot(squares[...], band[...], preferred_element_type=jnp.float32)
        energy = lax.rsqrt(energy + EPS)
        for p in range(4):
            inv[c + p] = energy[p * ROWS : (p + 1) * ROWS, :]

    def arrive(d, carry):
        owner = source(d)

        @pl.when(d > 0)
        def _():
            data(d, owner).wait_recv()

        energies(owner * CAP)
        energies(owner * CAP + 4)
        return carry

    lax.fori_loop(0, count, arrive, 0)

    edge = lax.broadcasted_iota(jnp.int32, (LAG_BLOCKS, LANES), 1)

    def apply(s, rolled):
        row = row_ref[s]
        move = move_ref[s]
        coarse = move // LANES
        fine = move % LANES
        frame = jnp.concatenate(
            [wave32[row, a : a + ROWS, : min(LANES, DEPTH - a * LANES)] for a in range(SPAN)], axis=1
        ).astype(jnp.bfloat16)
        corr = jnp.dot(frame, toep[s], preferred_element_type=jnp.float32)
        normed = corr * jnp.broadcast_to(norm[pl.ds(s, 1), :], corr.shape) * inv[row]
        normed = normed.astype(jnp.bfloat16).astype(jnp.float32)
        rolled[...] = pltpu.roll(normed, (LANES - fine) % LANES, 1)
        near_rows = rolled[pl.ds(coarse, LAG_BLOCKS), :]
        far_rows = rolled[pl.ds(coarse + 1, LAG_BLOCKS), :]
        ncc[pl.ds(s * PITCH, LAG_BLOCKS), :] = jnp.where(edge < LANES - fine, near_rows, far_rows)

    def apply_group(i, carry):
        for p, rolled in enumerate((roll0, roll1, roll2, roll3)):
            apply(4 * i + p, rolled)
        return carry

    lax.fori_loop(0, slots // 4, apply_group, 0)

    names = lax.broadcasted_iota(jnp.int32, (TPL_DEV, slots), 0)
    label[...] = jnp.where(names == jnp.broadcast_to(tmpl_ref[...], (TPL_DEV, slots)), 1.0, 0.0).astype(jnp.bfloat16)

    def block(other, side, q):
        at = (other * 2 + (core + side) % 2) * 8 + q
        picked = ncc[pl.ds(at, slots, stride=PITCH), :].astype(jnp.bfloat16)
        return jnp.dot(label[...], picked, preferred_element_type=jnp.float32)

    others = [(z + step) % 4 for step in steps] + [z]
    firsts = []
    for n, other in enumerate(others):
        for q in range(8):
            near_out[n, q] = block(other, 1, q).astype(jnp.bfloat16)
        copy = pltpu.make_async_remote_copy(
            src_ref=near_out.at[n],
            dst_ref=near.at[n],
            send_sem=near_send.at[n],
            recv_sem=near_recv.at[n],
            device_id={"sta": partner},
            device_id_type=MESH,
        )
        copy.start()
        firsts.append(copy)
    seconds = []
    for n, other in enumerate(others):
        for q in range(8):
            keep[q] = block(other, 0, q)
        firsts[n].wait_recv()
        if n == 3:
            break
        for q in range(8):
            far_out[n, q] = (keep[q] + near[n, q].astype(jnp.float32)).astype(jnp.bfloat16)
        copy = pltpu.make_async_remote_copy(
            src_ref=far_out.at[n],
            dst_ref=far.at[n],
            send_sem=far_send.at[n],
            recv_sem=far_recv.at[n],
            device_id={"sta": other * 2 + core},
            device_id_type=MESH,
        )
        copy.start()
        seconds.append(copy)
    for q in range(8):
        keep[q] = keep[q] + near[3, q].astype(jnp.float32)
    for d in range(1, count):
        data(d, me).wait_send()
    for copy in firsts:
        copy.wait_send()
    for copy in seconds:
        copy.wait()
    for q in range(8):
        total = keep[q]
        for n in range(3):
            total = total + far[n, q].astype(jnp.float32)
        out_ref[q * LANES : (q + 1) * LANES, :] = total.T


def stack_all(request, rows, moveouts, waves, taps, templates):
    slots = taps.shape[0]
    owners = lax.axis_size("tmpl")
    channels = owners * CAP
    waves = waves.reshape(waves.shape[0], BLOCKS, LANES)
    wide = jnp.broadcast_to(request[None, :], (8, channels))
    vmem = pl.BlockSpec(memory_space=pltpu.VMEM)
    smem = pl.BlockSpec(memory_space=pltpu.SMEM)
    f32, bf16 = jnp.float32, jnp.bfloat16
    dma = pltpu.SemaphoreType.DMA
    return pl.pallas_call(
        stack_kernel,
        out_shape=jax.ShapeDtypeStruct((8 * LANES, TPL_DEV), f32),
        in_specs=[smem, smem, smem, vmem, vmem, vmem, vmem],
        out_specs=vmem,
        scratch_shapes=[
            pltpu.VMEM((owners, 8, LANES), jnp.int32),
            pltpu.VMEM((owners, CAP, BLOCKS, LANES), bf16),
            pltpu.VMEM((channels, BLOCKS, LANES), bf16),
            pltpu.VMEM((channels, ROWS + 8, LANES), f32),
            pltpu.VMEM((channels, ROWS, LANES), f32),
            pltpu.VMEM((DEPTH, LANES), bf16),
            pltpu.VMEM((4, slots, LANES), f32),
            pltpu.VMEM((slots, LANES), f32),
            pltpu.VMEM((slots, DEPTH, LANES), bf16),
            pltpu.VMEM((4 * ROWS, DEPTH), bf16),
            pltpu.VMEM((ROWS, LANES), f32),
            pltpu.VMEM((ROWS, LANES), f32),
            pltpu.VMEM((ROWS, LANES), f32),
            pltpu.VMEM((ROWS, LANES), f32),
            pltpu.VMEM((slots * PITCH, LANES), f32),
            pltpu.VMEM((TPL_DEV, slots), bf16),
            pltpu.VMEM((4, 8, TPL_DEV, LANES), bf16),
            pltpu.VMEM((4, 8, TPL_DEV, LANES), bf16),
            pltpu.VMEM((3, 8, TPL_DEV, LANES), bf16),
            pltpu.VMEM((3, 8, TPL_DEV, LANES), bf16),
            pltpu.VMEM((8, TPL_DEV, LANES), f32),
            pltpu.SMEM((owners, 8, LANES), jnp.int32),
            dma((owners,)),
            dma((owners,)),
            dma((owners,)),
            dma((owners,)),
            dma((4,)),
            dma((4,)),
            dma((3,)),
            dma((3,)),
            dma,
        ],
        compiler_params=pltpu.CompilerParams(collective_id=0, has_side_effects=True, vmem_limit_bytes=67043328),
        name="stack",
    )(wide, rows, moveouts, wide, waves, taps, templates[None, :])


def per_device(waveforms, template_taps, slot_template, slot_channel, slot_moveout):
    groups = lax.axis_size("sta")
    owners = lax.axis_size("tmpl")
    request, rows = plan_rows(slot_channel, waveforms.shape[0], owners, groups)
    return stack_all(request, rows, slot_moveout, waveforms, template_taps, slot_template)


def solution(mesh):
    return jax.shard_map(
        per_device,
        mesh=mesh,
        in_specs=(
            P(("tmpl", "sta"), None),
            P(("tmpl", "sta"), None),
            P(("tmpl", "sta")),
            P(("tmpl", "sta")),
            P(("tmpl", "sta")),
        ),
        out_specs=P("sta", "tmpl"),
        check_vma=False,
    )
```

```python
import functools
import math

import jax
import jax.numpy as jnp
from jax import lax
from jax.experimental import pallas as pl
from jax.experimental.pallas import tpu as pltpu
from jax.sharding import PartitionSpec as P

TAPS = 400
CH_TPL = 30
LAGS = 8192
TPL_DEV = 128
CAP = 8
EPS = 1e-06
SCALE = math.sqrt(TAPS / CH_TPL)
LANES = 128
SPAN = 5
HALF = 256
DEPTH = HALF + 16
LAG_BLOCKS = LAGS // LANES
BLOCKS = 71
ROWS = 72
PITCH = LAG_BLOCKS + 1
EARLY = 32
GROUP = 8
BUILD = 2
MESH = pl.DeviceIdType.MESH


def plan_rows(slot_channel, channels_here, owners, groups):
    owner = slot_channel // channels_here // groups
    local = slot_channel % channels_here
    key = owner * channels_here + local
    count = key.shape[0]
    order = jnp.arange(count, dtype=jnp.int32)
    earlier = (key[:, None] == key[None, :]) & (order[None, :] < order[:, None])
    first = ~jnp.any(earlier, axis=1)
    below = (owner[:, None] == owner[None, :]) & (key[None, :] < key[:, None]) & first[None, :]
    row = owner * CAP + jnp.sum(below.astype(jnp.int32), axis=1)
    hit = (row[:, None] == jnp.arange(owners * CAP, dtype=jnp.int32)[None, :]) & first[:, None]
    request = jnp.sum(jnp.where(hit, local[:, None], 0), axis=0)
    return request, row


def stack_kernel(
    req_smem, row_ref, move_ref, req_ref, wave_ref, taps_ref, tmpl_ref, out_ref,
    req_all, send, recv, wave32, inv, band, flipped, norm, toep, squares, lows, head, tail, rolls, ncc, label,
    near_out, near, far_out, far, keep, req_here,
    req_send, req_recv, data_send, data_recv, near_send, near_recv, far_send, far_recv, local_sem,
):
    slots = taps_ref.shape[0]
    me = lax.axis_index("tmpl")
    x, y = me // 4, me % 4
    group = lax.axis_index("sta")
    z, core = group // 2, group % 2
    partner = z * 2 + (core + 1) % 2
    steps = (2, 1, 3)
    count = 16

    def peer(d):
        return ((x + d // 4) % 4) * 4 + (y + d % 4) % 4

    def source(d):
        return ((x + 4 - d // 4) % 4) * 4 + (y + 4 - d % 4) % 4

    barrier = pltpu.get_barrier_semaphore()
    for d in range(1, count):
        pl.semaphore_signal(barrier, inc=1, device_id={"tmpl": peer(d)}, device_id_type=MESH)
    for other in [partner] + [((z + step) % 4) * 2 + core for step in steps]:
        pl.semaphore_signal(barrier, inc=1, device_id={"sta": other}, device_id_type=MESH)

    sub = lax.broadcasted_iota(jnp.int32, (LANES, LANES), 0)
    lane = lax.broadcasted_iota(jnp.int32, (LANES, LANES), 1)
    flip = jnp.where(sub == (LANES - lane) % LANES, 1.0, 0.0).astype(jnp.bfloat16)
    power = jnp.zeros((slots, 1), jnp.float32)
    for b in range(4):
        piece = taps_ref[:, b * LANES : min(b * LANES + LANES, TAPS)]
        wide = piece.shape[1]
        flipped[b] = jnp.dot(piece, flip[:wide, :], preferred_element_type=jnp.float32)
        piece = piece.astype(jnp.float32)
        power = power + jnp.sum(piece * piece, axis=1, keepdims=True)
    norm[...] = jnp.broadcast_to(SCALE * lax.rsqrt(power + EPS), (slots, LANES))
    pl.semaphore_wait(barrier, count - 1 + 4)

    def ask(d):
        return pltpu.make_async_remote_copy(
            src_ref=req_ref,
            dst_ref=req_all.at[d],
            send_sem=req_send.at[d],
            recv_sem=req_recv.at[d],
            device_id={"tmpl": peer(d)},
            device_id_type=MESH,
        )

    for d in range(1, count):
        ask(d).start()

    lower = lax.broadcasted_iota(jnp.int16, (LANES, LANES), 1) <= lax.broadcasted_iota(jnp.int16, (LANES, LANES), 0)

    def build(s):
        last = jnp.zeros((LANES, LANES), jnp.bfloat16)
        for b in range(4):
            base = jnp.broadcast_to(flipped[b, pl.ds(s, 1), :], (16, LANES))
            base = pltpu.roll(base, 0, 1, stride=1, stride_axis=0).astype(jnp.bfloat16)
            circ = jnp.concatenate([base if g == 0 else pltpu.roll(base, 16 * g, 1) for g in range(8)], axis=0)
            down, across = b % 2 * LANES, b // 2 * LANES
            toep[s, down : down + LANES, across : across + LANES] = jnp.where(lower, circ, last)
            last = circ
        tail = DEPTH - HALF
        toep[s, HALF:, :LANES] = jnp.where(lower[:tail], jnp.zeros((tail, LANES), jnp.bfloat16), last[:tail])
        toep[s, HALF:, LANES:] = jnp.zeros((tail, LANES), jnp.bfloat16)

    def build_pair(i, carry):
        for p in range(BUILD):
            build(BUILD * i + p)
        return carry

    lax.fori_loop(0, EARLY // BUILD, build_pair, 0)

    for k in range(CAP):
        recv[me * CAP + k] = wave_ref[req_smem[0, me * CAP + k]]
    for d in range(1, count):
        ask(d).wait()
    here = pltpu.make_async_copy(req_all, req_here, local_sem)
    here.start()
    here.wait()

    def data(d, owner):
        return pltpu.make_async_remote_copy(
            src_ref=send.at[d],
            dst_ref=recv.at[pl.ds(owner * CAP, CAP)],
            send_sem=data_send.at[d],
            recv_sem=data_recv.at[d],
            device_id={"tmpl": peer(d)},
            device_id_type=MESH,
        )

    for d in range(1, count):
        back = (4 - d // 4) % 4 * 4 + (4 - d % 4) % 4
        for k in range(CAP):
            send[d, k] = wave_ref[req_here[back, 0, me * CAP + k]]
        data(d, me).start()

    lax.fori_loop(EARLY // BUILD, slots // BUILD, build_pair, 0)

    column = lax.broadcasted_iota(jnp.int32, (DEPTH, HALF), 0)
    across = lax.broadcasted_iota(jnp.int32, (DEPTH, HALF), 1)
    column = jnp.where(column < HALF, column + across // LANES * HALF, column + HALF + across // LANES * HALF)
    lagged = across % LANES
    band[...] = jnp.where((column >= lagged) & (column < lagged + TAPS), 1.0, 0.0).astype(jnp.bfloat16)
    wave32[:, ROWS:, :] = jnp.zeros((wave32.shape[0], wave32.shape[1] - ROWS, LANES), jnp.float32)

    parts = ((0, 0, LANES), (1, LANES, LANES), (4, HALF, DEPTH - HALF))

    def energies(c, squares, lows):
        for p in range(4):
            wave32[c + p, :BLOCKS, :] = recv[c + p].astype(jnp.float32)
            for a, at, width in parts:
                frame = wave32[c + p, a : a + ROWS, :width].astype(jnp.bfloat16)
                squares[p * ROWS : (p + 1) * ROWS, at : at + width] = frame * frame
        energy = jnp.dot(squares[...], band[...], preferred_element_type=jnp.float32)
        lows[...] = energy[:, LANES:]
        for p in range(4):
            inv[c + p, : ROWS - 2] = lax.rsqrt(energy[p * ROWS : (p + 1) * ROWS - 2, :LANES] + lows[p * ROWS + 2 : (p + 1) * ROWS, :] + EPS)

    def arrive(d, carry):
        owner = source(d)

        @pl.when(d > 0)
        def _():
            data(d, owner).wait_recv()

        for h in range(2):
            energies(owner * CAP + 4 * h, squares[h], lows[h])
        return carry

    lax.fori_loop(0, count, arrive, 0)

    edge = lax.broadcasted_iota(jnp.int32, (LAG_BLOCKS, LANES), 1)

    def product(s, p):
        row = row_ref[s]
        frame = jnp.concatenate([wave32[row, a : a + ROWS, :width] for a, at, width in parts], axis=1).astype(jnp.bfloat16)
        corr = jnp.dot(frame, toep[s], preferred_element_type=jnp.float32)
        head[p][...] = corr[:, :LANES]
        tail[p][:ROWS, :] = corr[:, LANES:]

    def settle(s, p):
        row = row_ref[s]
        move = move_ref[s]
        coarse = move // LANES
        fine = move % LANES
        corr = head[p][...] + tail[p][2 : ROWS + 2, :]
        normed = corr * jnp.broadcast_to(norm[pl.ds(s, 1), :], corr.shape) * inv[row]
        normed = normed.astype(jnp.bfloat16).astype(jnp.float32)
        rolled = rolls[p]
        rolled[...] = pltpu.roll(normed, (LANES - fine) % LANES, 1)
        near_rows = rolled[pl.ds(coarse, LAG_BLOCKS), :]
        far_rows = rolled[pl.ds(coarse + 1, LAG_BLOCKS), :]
        ncc[pl.ds(s * PITCH, LAG_BLOCKS), :] = jnp.where(edge < LANES - fine, near_rows, far_rows)

    for p in range(GROUP):
        product(p, p)

    def apply_group(i, carry):
        for p in range(GROUP):
            settle(GROUP * (i - 1) + p, p)
        for p in range(GROUP):
            product(GROUP * i + p, p)
        return carry

    lax.fori_loop(1, slots // GROUP, apply_group, 0)
    for p in range(GROUP):
        settle(slots - GROUP + p, p)

    names = lax.broadcasted_iota(jnp.int32, (TPL_DEV, slots), 0)
    label[...] = jnp.where(names == jnp.broadcast_to(tmpl_ref[...], (TPL_DEV, slots)), 1.0, 0.0).astype(jnp.bfloat16)

    def block(other, side, q):
        at = (other * 2 + (core + side) % 2) * 8 + 2 * q
        picked = jnp.concatenate([ncc[pl.ds(at + e, slots, stride=PITCH), :] for e in range(2)], axis=1).astype(jnp.bfloat16)
        return jnp.dot(label[...], picked, preferred_element_type=jnp.float32)

    others = [(z + step) % 4 for step in steps] + [z]
    firsts = []
    for n, other in enumerate(others):

        def outside(q, carry):
            total = block(other, 1, q).astype(jnp.bfloat16)
            near_out[n, 2 * q] = total[:, :LANES]
            near_out[n, 2 * q + 1] = total[:, LANES:]
            return carry

        lax.fori_loop(0, 4, outside, 0)
        copy = pltpu.make_async_remote_copy(
            src_ref=near_out.at[n],
            dst_ref=near.at[n],
            send_sem=near_send.at[n],
            recv_sem=near_recv.at[n],
            device_id={"sta": partner},
            device_id_type=MESH,
        )
        copy.start()
        firsts.append(copy)
    seconds = []
    for n, other in enumerate(others):
        firsts[n].wait_recv()

        def inside(q, carry):
            total = block(other, 0, q)
            for e in range(2):
                summed = total[:, e * LANES : (e + 1) * LANES] + near[n, 2 * q + e].astype(jnp.float32)
                if n == 3:
                    keep[2 * q + e] = summed
                else:
                    far_out[n, 2 * q + e] = summed.astype(jnp.bfloat16)
            return carry

        lax.fori_loop(0, 4, inside, 0)
        if n == 3:
            break
        copy = pltpu.make_async_remote_copy(
            src_ref=far_out.at[n],
            dst_ref=far.at[n],
            send_sem=far_send.at[n],
            recv_sem=far_recv.at[n],
            device_id={"sta": other * 2 + core},
            device_id_type=MESH,
        )
        copy.start()
        seconds.append(copy)
    for d in range(1, count):
        data(d, me).wait_send()
    for copy in firsts:
        copy.wait_send()
    for copy in seconds:
        copy.wait()
    for q in range(8):
        total = keep[q]
        for n in range(3):
            total = total + far[n, q].astype(jnp.float32)
        out_ref[q * LANES : (q + 1) * LANES, :] = total.T


def stack_all(request, rows, moveouts, waves, taps, templates):
    slots = taps.shape[0]
    owners = lax.axis_size("tmpl")
    channels = owners * CAP
    waves = waves.reshape(waves.shape[0], BLOCKS, LANES)
    wide = jnp.broadcast_to(request[None, :], (8, channels))
    vmem = pl.BlockSpec(memory_space=pltpu.VMEM)
    smem = pl.BlockSpec(memory_space=pltpu.SMEM)
    f32, bf16 = jnp.float32, jnp.bfloat16
    dma = pltpu.SemaphoreType.DMA
    return pl.pallas_call(
        stack_kernel,
        out_shape=jax.ShapeDtypeStruct((8 * LANES, TPL_DEV), f32),
        in_specs=[smem, smem, smem, vmem, vmem, vmem, vmem],
        out_specs=vmem,
        scratch_shapes=[
            pltpu.VMEM((owners, 8, LANES), jnp.int32),
            pltpu.VMEM((owners, CAP, BLOCKS, LANES), bf16),
            pltpu.VMEM((channels, BLOCKS, LANES), bf16),
            pltpu.VMEM((channels, ROWS + 8, LANES), f32),
            pltpu.VMEM((channels, ROWS, LANES), f32),
            pltpu.VMEM((DEPTH, HALF), bf16),
            pltpu.VMEM((4, slots, LANES), f32),
            pltpu.VMEM((slots, LANES), f32),
            pltpu.VMEM((slots, DEPTH, HALF), bf16),
            [pltpu.VMEM((4 * ROWS, DEPTH), bf16)] * 2,
            [pltpu.VMEM((4 * ROWS, LANES), f32)] * 2,
            [pltpu.VMEM((ROWS, LANES), f32)] * GROUP,
            [pltpu.VMEM((ROWS + 8, LANES), f32)] * GROUP,
            [pltpu.VMEM((ROWS, LANES), f32)] * GROUP,
            pltpu.VMEM((slots * PITCH, LANES), f32),
            pltpu.VMEM((TPL_DEV, slots), bf16),
            pltpu.VMEM((4, 8, TPL_DEV, LANES), bf16),
            pltpu.VMEM((4, 8, TPL_DEV, LANES), bf16),
            pltpu.VMEM((3, 8, TPL_DEV, LANES), bf16),
            pltpu.VMEM((3, 8, TPL_DEV, LANES), bf16),
            pltpu.VMEM((8, TPL_DEV, LANES), f32),
            pltpu.SMEM((owners, 8, LANES), jnp.int32),
            dma((owners,)),
            dma((owners,)),
            dma((owners,)),
            dma((owners,)),
            dma((4,)),
            dma((4,)),
            dma((3,)),
            dma((3,)),
            dma,
        ],
        compiler_params=pltpu.CompilerParams(collective_id=0, has_side_effects=True, vmem_limit_bytes=67043328),
        name="stack",
    )(wide, rows, moveouts, wide, waves, taps, templates[None, :])


def per_device(waveforms, template_taps, slot_template, slot_channel, slot_moveout):
    groups = lax.axis_size("sta")
    owners = lax.axis_size("tmpl")
    request, rows = plan_rows(slot_channel, waveforms.shape[0], owners, groups)
    return stack_all(request, rows, slot_moveout, waveforms, template_taps, slot_template)


def solution(mesh):
    return jax.shard_map(
        per_device,
        mesh=mesh,
        in_specs=(
            P(("tmpl", "sta"), None),
            P(("tmpl", "sta"), None),
            P(("tmpl", "sta")),
            P(("tmpl", "sta")),
            P(("tmpl", "sta")),
        ),
        out_specs=P("sta", "tmpl"),
        check_vma=False,
    )
```

```python
import functools
import math

import jax
import jax.numpy as jnp
from jax import lax
from jax.experimental import pallas as pl
from jax.experimental.pallas import tpu as pltpu
from jax.sharding import PartitionSpec as P

TAPS = 400
CH_TPL = 30
LAGS = 8192
TPL_DEV = 128
CAP = 8
EPS = 1e-06
SCALE = math.sqrt(TAPS / CH_TPL)
LANES = 128
SPAN = 5
HALF = 256
DEPTH = HALF + 16
LAG_BLOCKS = LAGS // LANES
BLOCKS = 71
ROWS = 72
CHUNK = 16
PITCH = CHUNK + 1
WINDOW = 24
PARTS = (0, 32, 48, 64, 72)
EARLY = 32
GROUP = 8
BUILD = 2
MESH = pl.DeviceIdType.MESH


def plan_rows(slot_channel, channels_here, owners, groups):
    owner = slot_channel // channels_here // groups
    local = slot_channel % channels_here
    key = owner * channels_here + local
    count = key.shape[0]
    order = jnp.arange(count, dtype=jnp.int32)
    earlier = (key[:, None] == key[None, :]) & (order[None, :] < order[:, None])
    first = ~jnp.any(earlier, axis=1)
    below = (owner[:, None] == owner[None, :]) & (key[None, :] < key[:, None]) & first[None, :]
    row = owner * CAP + jnp.sum(below.astype(jnp.int32), axis=1)
    hit = (row[:, None] == jnp.arange(owners * CAP, dtype=jnp.int32)[None, :]) & first[:, None]
    request = jnp.sum(jnp.where(hit, local[:, None], 0), axis=0)
    return request, row


def stack_kernel(
    req_smem, row_ref, move_ref, req_ref, wave_ref, taps_ref, tmpl_ref, out_ref,
    req_all, turned, send, recv, wave32, inv, band, flipped, norm, toep, squares, lows, head, tail, rolls, ncc, label,
    near_out, near, far_out, far, keep, req_here,
    req_send, req_recv, data_send, data_recv, near_send, near_recv, far_send, far_recv, local_sem,
):
    slots = taps_ref.shape[0]
    me = lax.axis_index("tmpl")
    x, y = me // 4, me % 4
    group = lax.axis_index("sta")
    z, core = group // 2, group % 2
    partner = z * 2 + (core + 1) % 2
    steps = (2, 1, 3)
    count = 16

    def peer(d):
        return ((x + d // 4) % 4) * 4 + (y + d % 4) % 4

    def source(d):
        return ((x + 4 - d // 4) % 4) * 4 + (y + 4 - d % 4) % 4

    barrier = pltpu.get_barrier_semaphore()
    for d in range(1, count):
        pl.semaphore_signal(barrier, inc=1, device_id={"tmpl": peer(d)}, device_id_type=MESH)
    for other in [partner] + [((z + step) % 4) * 2 + core for step in steps]:
        pl.semaphore_signal(barrier, inc=1, device_id={"sta": other}, device_id_type=MESH)

    sub = lax.broadcasted_iota(jnp.int32, (LANES, LANES), 0)
    lane = lax.broadcasted_iota(jnp.int32, (LANES, LANES), 1)
    flip = jnp.where(sub == (LANES - lane) % LANES, 1.0, 0.0).astype(jnp.bfloat16)
    power = jnp.zeros((slots, 1), jnp.float32)
    for b in range(4):
        piece = taps_ref[:, b * LANES : min(b * LANES + LANES, TAPS)]
        wide = piece.shape[1]
        flipped[b] = jnp.dot(piece, flip[:wide, :], preferred_element_type=jnp.float32)
        piece = piece.astype(jnp.float32)
        power = power + jnp.sum(piece * piece, axis=1, keepdims=True)
    norm[...] = jnp.broadcast_to(SCALE * lax.rsqrt(power + EPS), (slots, LANES))
    lead = (z + 1) % 4
    turns = []
    for i in range(9):
        turn = 2 * lead + i
        turns.append(pl.multiple_of(jnp.where(turn >= 9, turn - 9, turn) * 8, 8))

    def rotate(c, carry):
        for i in range(9):
            turned[c, 8 * i : 8 * i + 8, :] = wave_ref[c, pl.ds(turns[i], 8), :]
        return carry

    lax.fori_loop(0, turned.shape[0], rotate, 0)
    pl.semaphore_wait(barrier, count - 1 + 4)

    def ask(d):
        return pltpu.make_async_remote_copy(
            src_ref=req_ref,
            dst_ref=req_all.at[d],
            send_sem=req_send.at[d],
            recv_sem=req_recv.at[d],
            device_id={"tmpl": peer(d)},
            device_id_type=MESH,
        )

    for d in range(1, count):
        ask(d).start()

    lower = lax.broadcasted_iota(jnp.int16, (LANES, LANES), 1) <= lax.broadcasted_iota(jnp.int16, (LANES, LANES), 0)

    def build(s):
        last = jnp.zeros((LANES, LANES), jnp.bfloat16)
        for b in range(4):
            base = jnp.broadcast_to(flipped[b, pl.ds(s, 1), :], (16, LANES))
            base = pltpu.roll(base, 0, 1, stride=1, stride_axis=0).astype(jnp.bfloat16)
            circ = jnp.concatenate([base if g == 0 else pltpu.roll(base, 16 * g, 1) for g in range(8)], axis=0)
            down, across = b % 2 * LANES, b // 2 * LANES
            toep[s, down : down + LANES, across : across + LANES] = jnp.where(lower, circ, last)
            last = circ
        tail = DEPTH - HALF
        toep[s, HALF:, :LANES] = jnp.where(lower[:tail], jnp.zeros((tail, LANES), jnp.bfloat16), last[:tail])
        toep[s, HALF:, LANES:] = jnp.zeros((tail, LANES), jnp.bfloat16)

    def build_pair(i, carry):
        for p in range(BUILD):
            build(BUILD * i + p)
        return carry

    lax.fori_loop(0, EARLY // BUILD, build_pair, 0)

    for k in range(CAP):
        recv[me * CAP + k] = turned[req_smem[0, me * CAP + k]]
    for d in range(1, count):
        ask(d).wait()
    here = pltpu.make_async_copy(req_all, req_here, local_sem)
    here.start()
    here.wait()

    def data(d, part, owner):
        rows = pl.ds(PARTS[part], PARTS[part + 1] - PARTS[part])
        return pltpu.make_async_remote_copy(
            src_ref=send.at[d, :, rows],
            dst_ref=recv.at[pl.ds(owner * CAP, CAP), rows],
            send_sem=data_send.at[d, part],
            recv_sem=data_recv.at[d, part],
            device_id={"tmpl": peer(d)},
            device_id_type=MESH,
        )

    for d in range(1, count):
        back = (4 - d // 4) % 4 * 4 + (4 - d % 4) % 4
        for k in range(CAP):
            send[d, k] = turned[req_here[back, 0, me * CAP + k]]
        data(d, 0, me).start()
    for part in range(1, 4):
        for d in range(1, count):
            data(d, part, me).start()

    names = lax.broadcasted_iota(jnp.int32, (TPL_DEV, slots), 0)
    label[...] = jnp.where(names == jnp.broadcast_to(tmpl_ref[...], (TPL_DEV, slots)), 1.0, 0.0).astype(jnp.bfloat16)

    lax.fori_loop(EARLY // BUILD, slots // BUILD, build_pair, 0)

    column = lax.broadcasted_iota(jnp.int32, (DEPTH, HALF), 0)
    across = lax.broadcasted_iota(jnp.int32, (DEPTH, HALF), 1)
    column = jnp.where(column < HALF, column + across // LANES * HALF, column + HALF + across // LANES * HALF)
    lagged = across % LANES
    band[...] = jnp.where((column >= lagged) & (column < lagged + TAPS), 1.0, 0.0).astype(jnp.bfloat16)
    wave32[:, ROWS + 8 :, :] = jnp.zeros((wave32.shape[0], 8, LANES), jnp.float32)
    parts = ((0, 0, LANES), (1, LANES, LANES), (4, HALF, DEPTH - HALF))
    edge = lax.broadcasted_iota(jnp.int32, (CHUNK, LANES), 1)

    def prepare(part, base):
        rows = slice(PARTS[part], PARTS[part + 1])

        def arrive(d, carry):
            data(d, part, source(d)).wait_recv()
            return carry

        lax.fori_loop(1, count, arrive, 0)

        def settle_pair(i, carry):
            for h in range(2):
                c = (2 * i + h) * CAP
                for p in range(CAP):
                    wave32[c + p, rows, :] = recv[c + p, rows, :].astype(jnp.float32)
                    if part == 3:
                        wave32[c + p, ROWS : ROWS + 8, :] = recv[c + p, :8, :].astype(jnp.float32)
            for h in range(2):
                c = (2 * i + h) * CAP
                for p in range(CAP):
                    for a, at, width in parts:
                        frame = wave32[c + p, pl.ds(base + a, WINDOW), :width].astype(jnp.bfloat16)
                        squares[h][p * WINDOW : (p + 1) * WINDOW, at : at + width] = frame * frame
            for h in range(2):
                c = (2 * i + h) * CAP
                energy = jnp.dot(squares[h][...], band[...], preferred_element_type=jnp.float32)
                lows[h][: CAP * WINDOW, :] = energy[:, LANES:]
                energy = energy[:, :LANES] + lows[h][2 : CAP * WINDOW + 2, :]
                energy = lax.rsqrt(energy + EPS)
                for p in range(CAP):
                    inv[c + p] = energy[p * WINDOW : (p + 1) * WINDOW, :]
            return carry

        lax.fori_loop(0, count // 2, settle_pair, 0)

    def correlate(base):
        def product(s, p):
            row = row_ref[s]
            frame = jnp.concatenate(
                [wave32[row, pl.ds(base + a, WINDOW), :width] for a, at, width in parts], axis=1
            ).astype(jnp.bfloat16)
            corr = jnp.dot(frame, toep[s], preferred_element_type=jnp.float32)
            head[p][...] = corr[:, :LANES]
            tail[p][:WINDOW, :] = corr[:, LANES:]

        def settle(s, p):
            row = row_ref[s]
            move = move_ref[s]
            coarse = lax.shift_right_logical(move, 7)
            fine = move & 127
            corr = head[p][...] + tail[p][2 : WINDOW + 2, :]
            normed = corr * jnp.broadcast_to(norm[pl.ds(s, 1), :], corr.shape) * inv[row]
            normed = normed.astype(jnp.bfloat16).astype(jnp.float32)
            rolled = rolls[p]
            rolled[...] = pltpu.roll(normed, (LANES - fine) & 127, 1)
            near_rows = rolled[pl.ds(coarse, CHUNK), :]
            far_rows = rolled[pl.ds(coarse + 1, CHUNK), :]
            ncc[pl.ds(s * PITCH, CHUNK), :] = jnp.where(edge < LANES - fine, near_rows, far_rows)

        for p in range(GROUP):
            product(p, p)

        def apply_group(i, carry):
            for p in range(GROUP):
                settle(GROUP * (i - 1) + p, p)
            for p in range(GROUP):
                product(GROUP * i + p, p)
            return carry

        lax.fori_loop(1, slots // GROUP, apply_group, 0)
        for p in range(GROUP):
            settle(slots - GROUP + p, p)

    def block(side, q):
        at = (core + side) % 2 * 8 + 2 * q
        picked = jnp.concatenate([ncc[pl.ds(at + e, slots, stride=PITCH), :] for e in range(2)], axis=1).astype(jnp.bfloat16)
        return jnp.dot(label[...], picked, preferred_element_type=jnp.float32)

    def near_copy(j):
        return pltpu.make_async_remote_copy(
            src_ref=near_out.at[j],
            dst_ref=near.at[j],
            send_sem=near_send.at[j],
            recv_sem=near_recv.at[j],
            device_id={"sta": partner},
            device_id_type=MESH,
        )

    def far_copy(j):
        return pltpu.make_async_remote_copy(
            src_ref=far_out.at[j],
            dst_ref=far.at[j],
            send_sem=far_send.at[j],
            recv_sem=far_recv.at[j],
            device_id={"sta": (lead + j) % 4 * 2 + core},
            device_id_type=MESH,
        )

    def gather(j):
        def outside(q, carry):
            total = block(1, q).astype(jnp.bfloat16)
            near_out[j, 2 * q] = total[:, :LANES]
            near_out[j, 2 * q + 1] = total[:, LANES:]
            return carry

        lax.fori_loop(0, 4, outside, 0)
        near_copy(j).start()

        def inside(q, carry):
            total = block(0, q)
            keep[j, 2 * q] = total[:, :LANES]
            keep[j, 2 * q + 1] = total[:, LANES:]
            return carry

        lax.fori_loop(0, 4, inside, 0)

    def forward(j):
        near_copy(j).wait_recv()
        for q in range(8):
            far_out[j, q] = (keep[j, q] + near[j, q].astype(jnp.float32)).astype(jnp.bfloat16)
        far_copy(j).start()

    for j in range(4):
        base = pl.multiple_of(16 * j + jnp.where(lead + j >= 4, 8, 0), 8)
        prepare(j, base)
        if j > 0:
            forward(j - 1)
        correlate(base)
        gather(j)
    near_copy(3).wait_recv()
    for q in range(8):
        keep[3, q] = keep[3, q] + near[3, q].astype(jnp.float32)
    for part in range(4):
        for d in range(1, count):
            data(d, part, me).wait_send()
        near_copy(part).wait_send()
    for j in range(3):
        far_copy(j).wait()
    for q in range(8):
        total = keep[3, q]
        for j in range(3):
            total = total + far[j, q].astype(jnp.float32)
        out_ref[q * LANES : (q + 1) * LANES, :] = total.T


def stack_all(request, rows, moveouts, waves, taps, templates):
    slots = taps.shape[0]
    owners = lax.axis_size("tmpl")
    channels = owners * CAP
    waves = jnp.pad(waves.reshape(waves.shape[0], BLOCKS, LANES), ((0, 0), (0, ROWS - BLOCKS), (0, 0)))
    wide = jnp.broadcast_to(request[None, :], (8, channels))
    vmem = pl.BlockSpec(memory_space=pltpu.VMEM)
    smem = pl.BlockSpec(memory_space=pltpu.SMEM)
    f32, bf16 = jnp.float32, jnp.bfloat16
    dma = pltpu.SemaphoreType.DMA
    return pl.pallas_call(
        stack_kernel,
        out_shape=jax.ShapeDtypeStruct((8 * LANES, TPL_DEV), f32),
        in_specs=[smem, smem, smem, vmem, vmem, vmem, vmem],
        out_specs=vmem,
        scratch_shapes=[
            pltpu.VMEM((owners, 8, LANES), jnp.int32),
            pltpu.VMEM(waves.shape, bf16),
            pltpu.VMEM((owners, CAP, ROWS, LANES), bf16),
            pltpu.VMEM((channels, ROWS, LANES), bf16),
            pltpu.VMEM((channels, ROWS + 16, LANES), f32),
            pltpu.VMEM((channels, WINDOW, LANES), f32),
            pltpu.VMEM((DEPTH, HALF), bf16),
            pltpu.VMEM((4, slots, LANES), f32),
            pltpu.VMEM((slots, LANES), f32),
            pltpu.VMEM((slots, DEPTH, HALF), bf16),
            [pltpu.VMEM((CAP * WINDOW, DEPTH), bf16)] * 2,
            [pltpu.VMEM((CAP * WINDOW + 8, LANES), f32)] * 2,
            [pltpu.VMEM((WINDOW, LANES), f32)] * GROUP,
            [pltpu.VMEM((WINDOW + 8, LANES), f32)] * GROUP,
            [pltpu.VMEM((WINDOW, LANES), f32)] * GROUP,
            pltpu.VMEM((slots * PITCH, LANES), f32),
            pltpu.VMEM((TPL_DEV, slots), bf16),
            pltpu.VMEM((4, 8, TPL_DEV, LANES), bf16),
            pltpu.VMEM((4, 8, TPL_DEV, LANES), bf16),
            pltpu.VMEM((3, 8, TPL_DEV, LANES), bf16),
            pltpu.VMEM((3, 8, TPL_DEV, LANES), bf16),
            pltpu.VMEM((4, 8, TPL_DEV, LANES), f32),
            pltpu.SMEM((owners, 8, LANES), jnp.int32),
            dma((owners,)),
            dma((owners,)),
            dma((owners, 4)),
            dma((owners, 4)),
            dma((4,)),
            dma((4,)),
            dma((3,)),
            dma((3,)),
            dma,
        ],
        compiler_params=pltpu.CompilerParams(collective_id=0, has_side_effects=True, vmem_limit_bytes=67043328),
        name="stack",
    )(wide, rows, moveouts, wide, waves, taps, templates[None, :])


def per_device(waveforms, template_taps, slot_template, slot_channel, slot_moveout):
    groups = lax.axis_size("sta")
    owners = lax.axis_size("tmpl")
    request, rows = plan_rows(slot_channel, waveforms.shape[0], owners, groups)
    return stack_all(request, rows, slot_moveout, waveforms, template_taps, slot_template)


def solution(mesh):
    return jax.shard_map(
        per_device,
        mesh=mesh,
        in_specs=(
            P(("tmpl", "sta"), None),
            P(("tmpl", "sta"), None),
            P(("tmpl", "sta")),
            P(("tmpl", "sta")),
            P(("tmpl", "sta")),
        ),
        out_specs=P("sta", "tmpl"),
        check_vma=False,
    )
```
